32 devices in a mesh: grp: 2 (over x), row: 4 (over y, core), diag: 4 (over z).
Axes of the slice: x: 2, y: 2, z: 4, core: 2. Of those that a mesh axis runs over, the one named last changes fastest.
Arguments:
- emb_rows: bfloat16 [32, 1024], P(None, ('grp', 'row')), parts along dimension 1, may hold values from -6 to 6
- emb_cols: bfloat16 [32, 1024], P(None, ('grp', 'row')), parts along dimension 1, may hold values from -6 to 6
- kernel: bfloat16 [3, 3, 32, 32], replicated, may hold values from -0.375 to 0.375
- bias: float32 [32], replicated, may hold values from -3 to 3
- cotangent: bfloat16 [32, 1024, 512], P(None, ('grp', 'row'), 'diag'), parts along dimension 1, may hold values from -6 to 6
- valid: int32 [1024], P(('grp', 'row')), parts along dimension 0, may hold values 0 or 1
- dilation: int32 [2], P('grp'), parts along dimension 0, may hold values from 1 to 4
- band: int32 [2], P('grp'), parts along dimension 0, may hold values from 384 to 512
Outputs:
- pair_out: bfloat16 [32, 1024, 512], P(None, ('grp', 'row'), 'diag'), parts along dimension 1
- row_grad: float32 [32, 1024], P(None, ('grp', 'row')), parts along dimension 1
- col_grad: float32 [32, 1024], P(None, ('grp', 'row')), parts along dimension 1
- kernel_grad: float32 [6, 3, 32, 32], P('grp'), parts along dimension 0
- bias_grad: float32 [64], P('grp'), parts along dimension 0
The draws below stay inside these ranges and needn't reach their ends.
There are 2 independent parts, one for each index of `grp`. The reference program is written for one: setup_inputs(seed, part) draws one part's arguments, and reference() takes and returns one part's arrays. A program takes and returns all parts, laid end to end along the dimension named above; an argument that names none is the same for every part. Nothing has to cross between parts.
All inputs are finite; a program needn't handle non-finite values. No bound on the sum of `valid` on one device may be relied on, other than what follows from the above.
Results may differ from the reference program's by a relative error of at most 0.0032.
Values may be sent and summed in bfloat16 or wider, within the bound.
A program may use at most 128 MiB of HBM per device.

```python
import jax
import jax.numpy as jnp
from jax import lax

CH = 32
MAXDIL = 4
ROWS_DEV = 128
LENGTH = 512
DIAGONAL_COUNT = 512


def touch_ends(drawn, stream_key, low, high):
    spot = [jax.random.randint(jax.random.fold_in(stream_key, axis), (), 0, length) for axis, length in enumerate(drawn.shape)]
    widest = drawn.shape.index(max(drawn.shape))
    neighbour = spot[:widest] + [(spot[widest] + 1) % drawn.shape[widest]] + spot[widest + 1:]
    return drawn.at[tuple(spot)].set(low).at[tuple(neighbour)].set(high)


def steps_of(rng, extent, cuts, low, top_value):
    level, own = 1.0, jax.random.fold_in(rng, 6)
    for dim, shards_of in cuts:
        draws = jnp.exp(jax.random.uniform(jax.random.fold_in(own, dim), (shards_of,), jnp.float32, low / len(cuts), top_value / len(cuts)))
        level = level * jnp.repeat(draws, extent[dim] // shards_of).reshape([-1 if axis == dim else 1 for axis in range(len(extent))])
    return level


def scatter_about(own_key, extent, deviation, limit, split=(), held_as=jnp.bfloat16):
    values = jax.random.normal(own_key, extent, jnp.float32) * deviation
    if len(split) > 0:
        values = steps_of(own_key, extent, split, -0.22, 0.18) * values
    return jnp.clip(values, min=-limit, max=limit).astype(held_as)


def setup_inputs(seed: int = 0, part: int = 0) -> dict:
    arg_keys = jax.random.split(jax.random.key(seed), 9)
    own_keys = jax.random.split(jax.random.fold_in(arg_keys[8], part), 9)
    return {
        "emb_rows": scatter_about(own_keys[0], (CH, LENGTH), 1.0, 6.0, ((1, 4),)),
        "emb_cols": scatter_about(own_keys[1], (CH, LENGTH), 1.0, 6.0, ((1, 4),)),
        "kernel": scatter_about(arg_keys[2], (3, 3, CH, CH), (9 * CH) ** -0.5, 0.375),
        "bias": scatter_about(arg_keys[3], (CH,), 0.5, 3.0, (), jnp.float32),
        "cotangent": scatter_about(own_keys[4], (CH, LENGTH, DIAGONAL_COUNT), 1.0, 6.0, ((1, 4), (2, 4))),
        "valid": touch_ends((jax.random.randint(own_keys[5], (LENGTH,), 0, 10) < 9).astype(jnp.int32), jax.random.fold_in(own_keys[5], 1), 0, 1),
        "dilation": jax.random.randint(own_keys[6], (1,), 1, MAXDIL + 1).astype(jnp.int32),
        "band": jax.random.randint(own_keys[7], (1,), DIAGONAL_COUNT * 3 // 4, DIAGONAL_COUNT + 1).astype(jnp.int32),
    }


def diagonal_take(window, row_number, diagonal_number):
    span_width = row_number + diagonal_number - 1
    leading = window.shape[:-1]
    widened = jnp.broadcast_to(window[..., None, :], leading + (row_number, span_width))
    flattened = widened.reshape(leading + (row_number * span_width,))
    flattened = jnp.pad(flattened, [(0, 0)] * len(leading) + [(0, row_number)])
    return flattened.reshape(leading + (row_number, span_width + 1))[..., :diagonal_number]

def diagonal_fold(field):
    channels, row_number, diagonal_number = field.shape
    span_width = row_number + diagonal_number - 1
    padded = jnp.pad(field, ((0, 0), (0, 0), (0, span_width + 1 - diagonal_number)))
    flattened = padded.reshape(channels, row_number * (span_width + 1))[:, :row_number * span_width]
    return lax.optimization_barrier(jnp.sum(flattened.reshape(channels, row_number, span_width), axis=1))

def diagonal_sums(field):
    channels, row_number, diagonal_number = field.shape
    block_row_list = 128 if row_number % 128 == 0 else row_number
    part_width = block_row_list + diagonal_number - 1

    def accumulate(index, totals):
        first = index * block_row_list
        piece = lax.dynamic_slice_in_dim(field, first, block_row_list, 1)
        current = lax.dynamic_slice_in_dim(totals, first, part_width, 1)
        return lax.dynamic_update_slice_in_dim(totals, current + diagonal_fold(piece), first, 1)
    totals = jnp.zeros((channels, row_number + diagonal_number - 1), jnp.float32)
    return lax.fori_loop(0, row_number // block_row_list, accumulate, totals)

def pair_block(row_embed, row_valid, col_window, col_valid, first_diag, row_number, diagonal_number, band_limit):
    outer = row_embed.astype(jnp.float32)[:, :, None] + diagonal_take(col_window, row_number, diagonal_number).astype(jnp.float32)
    offsets = first_diag + jnp.arange(diagonal_number, dtype=jnp.int32)
    inside = ((offsets >= 0) & (offsets < band_limit)).astype(jnp.float32)
    validity = row_valid[:, None] * diagonal_take(col_valid[None], row_number, diagonal_number)[0] * inside[None, :]
    hidden = outer * validity
    active = (jax.nn.gelu(hidden) * validity).astype(jnp.bfloat16)
    return (hidden, validity, active)

def contract(form, left, right):
    return jnp.einsum(form, left.astype(jnp.float32), right.astype(jnp.float32))

def dilated_convolve(active_extended, kernel, dilation_factor, row_number, diagonal_number, border_width):
    channels = active_extended.shape[0]
    result = jnp.zeros((kernel.shape[2], row_number, diagonal_number), jnp.float32)
    for kernel_tap_row in range(3):
        for kernel_tap_column in range(3):
            corner_patch = (jnp.int32(0), border_width + (kernel_tap_row - 1) * dilation_factor, border_width + (kernel_tap_column - kernel_tap_row) * dilation_factor)
            piece = lax.dynamic_slice(active_extended, corner_patch, (channels, row_number, diagonal_number))
            result = result + contract('oc,crk->ork', kernel[kernel_tap_row, kernel_tap_column], piece)
    return result

def kernel_summands(gradient_local, active_extended, dilation_factor, row_number, diagonal_number, border_width):
    channels = active_extended.shape[0]
    taps = []
    for kernel_tap_row in range(3):
        for kernel_tap_column in range(3):
            corner_patch = (jnp.int32(0), border_width + (kernel_tap_row - 1) * dilation_factor, border_width + (kernel_tap_column - kernel_tap_row) * dilation_factor)
            piece = lax.dynamic_slice(active_extended, corner_patch, (channels, row_number, diagonal_number))
            taps.append(contract('ork,crk->oc', gradient_local, piece))
    return jnp.stack(taps).reshape(3, 3, channels, channels)

def dilated_convolve_grad(gradient_extended, kernel, dilation_factor, row_number, diagonal_number, border_width):
    channels = gradient_extended.shape[0]
    result = jnp.zeros((kernel.shape[3], row_number, diagonal_number), jnp.float32)
    for kernel_tap_row in range(3):
        for kernel_tap_column in range(3):
            corner_patch = (jnp.int32(0), border_width - (kernel_tap_row - 1) * dilation_factor, border_width - (kernel_tap_column - kernel_tap_row) * dilation_factor)
            piece = lax.dynamic_slice(gradient_extended, corner_patch, (channels, row_number, diagonal_number))
            result = result + contract('oc,ork->crk', kernel[kernel_tap_row, kernel_tap_column], piece)
    return result

def reference(emb_rows, emb_cols, kernel, bias, cotangent, valid, dilation, band):
    border_width = 2 * MAXDIL
    block_row_list = ROWS_DEV
    channels = emb_rows.shape[0]
    dilation_factor = dilation[0]
    band_limit = band[0]
    valid_float = valid.astype(jnp.float32)
    cols_padded = jnp.pad(emb_cols, ((0, 0), (2 * border_width, DIAGONAL_COUNT + 2 * border_width + block_row_list)))
    cvalid_padded = jnp.pad(valid_float, (2 * border_width, DIAGONAL_COUNT + 2 * border_width + block_row_list))
    rows_padded = jnp.pad(emb_rows, ((0, 0), (border_width, border_width)))
    rvalid_padded = jnp.pad(valid_float, (border_width, border_width))
    grad_padded = jnp.pad(cotangent, ((0, 0), (border_width, border_width), (border_width, border_width)))

    def advance(carry, block_index):
        col_totals, kernel_total, bias_total = carry
        first = block_index * block_row_list
        row_embed = lax.dynamic_slice_in_dim(rows_padded, first, block_row_list + 2 * border_width, 1)
        row_valid = lax.dynamic_slice_in_dim(rvalid_padded, first, block_row_list + 2 * border_width, 0)
        span = block_row_list + DIAGONAL_COUNT + 4 * border_width - 1
        col_window = lax.dynamic_slice_in_dim(cols_padded, first, span, 1)
        col_valid = lax.dynamic_slice_in_dim(cvalid_padded, first, span, 0)
        hidden_ext, valid_ext, active_extended = pair_block(row_embed, row_valid, col_window, col_valid, -border_width, block_row_list + 2 * border_width, DIAGONAL_COUNT + 2 * border_width, band_limit)
        hidden = hidden_ext[:, border_width:border_width + block_row_list, border_width:border_width + DIAGONAL_COUNT]
        validity = valid_ext[border_width:border_width + block_row_list, border_width:border_width + DIAGONAL_COUNT]
        mixed_features = dilated_convolve(active_extended, kernel, dilation_factor, block_row_list, DIAGONAL_COUNT, border_width) + bias[:, None, None]
        output = ((hidden + mixed_features) * validity).astype(jnp.bfloat16)
        corner_patch = (jnp.int32(0), first, jnp.int32(0))
        grad_window = lax.dynamic_slice(grad_padded, corner_patch, (channels, block_row_list + 2 * border_width, DIAGONAL_COUNT + 2 * border_width))
        gradient_extended = (grad_window.astype(jnp.float32) * valid_ext).astype(jnp.bfloat16)
        gradient_local = gradient_extended[:, border_width:border_width + block_row_list, border_width:border_width + DIAGONAL_COUNT]
        kernel_portion = kernel_summands(gradient_local, active_extended, dilation_factor, block_row_list, DIAGONAL_COUNT, border_width)
        bias_part = lax.optimization_barrier(jnp.sum(gradient_local.astype(jnp.float32), axis=(1, 2)))
        activation_grad = dilated_convolve_grad(gradient_extended, kernel, dilation_factor, block_row_list, DIAGONAL_COUNT, border_width)
        unused, pullback = jax.vjp(jax.nn.gelu, hidden)
        dpair = (gradient_local.astype(jnp.float32) + pullback(activation_grad * validity)[0]) * validity
        row_part = lax.optimization_barrier(jnp.sum(dpair, axis=2))
        col_part = diagonal_sums(dpair)
        current = lax.dynamic_slice_in_dim(col_totals, first, block_row_list + DIAGONAL_COUNT - 1, 1)
        col_totals = lax.dynamic_update_slice_in_dim(col_totals, current + col_part, first, 1)
        return ((col_totals, kernel_total + kernel_portion, bias_total + bias_part), (output, row_part))
    start = (jnp.zeros((channels, LENGTH + DIAGONAL_COUNT + block_row_list), jnp.float32), jnp.zeros((3, 3, channels, channels), jnp.float32), jnp.zeros((channels,), jnp.float32))
    count = LENGTH // block_row_list
    final, stacked = lax.scan(advance, start, jnp.arange(count, dtype=jnp.int32))
    col_totals, kernel_total, bias_total = final
    outputs, row_parts = stacked
    pair_out = jnp.transpose(outputs, (1, 0, 2, 3)).reshape(channels, LENGTH, DIAGONAL_COUNT)
    row_sum = jnp.transpose(row_parts, (1, 0, 2)).reshape(channels, LENGTH)
    embed_scale = 1.0 / jnp.sqrt(jnp.float32(DIAGONAL_COUNT))
    weight_scale = 1.0 / jnp.sqrt(jnp.float32(LENGTH) * jnp.float32(DIAGONAL_COUNT))
    return (pair_out, row_sum * embed_scale, col_totals[:, :LENGTH] * embed_scale, kernel_total * weight_scale, bias_total * weight_scale)
```

```python
import functools

import jax
import jax.numpy as jnp
from jax import lax
from jax.experimental import pallas as pl
from jax.experimental.pallas import tpu as pltpu
from jax.sharding import PartitionSpec as P

MAXDIL = 4
RG = 8
S2PI = 0.7978845608028654
CUBIC = 0.044715


def with_halo(array, axis, dim, width):
    size, length = (lax.axis_size(axis), array.shape[dim])
    up = [(i, i + 1) for i in range(size - 1)]
    down = [(j, i) for i, j in up]
    last = lax.slice_in_dim(array, length - width, length, axis=dim)
    initial = lax.slice_in_dim(array, 0, width, axis=dim)
    return lax.ppermute(last, axis, up), lax.ppermute(initial, axis, down)


def pair_kernel(
    par, vr, rows, cols, vcol, cot, halo, kf, kb, bias,
    out, rsum, csum, kgrad,
    act3, gz3, gzm, hid, der, tf, tb, kacc, bacc,
):
    n = out.shape[0]
    ch = out.shape[1]
    wide = 2 * n
    r, w, d0 = par[0], par[1], par[2]
    groups = n // RG
    blk = RG * ch
    lane1 = lax.broadcasted_iota(jnp.int32, (RG, wide), 1)

    def offsets(i):
        d = lane1 - i
        d = jnp.where(d < -(n // 2), d + wide, d)
        return jnp.where(d >= wide - n // 2, d - wide, d)

    def validity(e, i, side):
        d = offsets(i)
        inside = (d + d0 >= 0) & (d + d0 < w)
        v = jnp.where(inside, vcol[side] * vr[e], 0.0)
        return v, d

    kblk = lax.broadcasted_iota(jnp.int32, (ch, 2 * blk), 1) // ch
    for b in range(3):
        for ii in range(RG):
            f = jnp.zeros((ch, 2 * blk), jnp.float32)
            g = jnp.zeros((ch, 2 * blk), jnp.float32)
            for a in range(3):
                f = jnp.where(kblk == ii + MAXDIL + (a - 1) * r, kf[3 * a + b].astype(jnp.float32), f)
                g = jnp.where(kblk == ii + MAXDIL - (a - 1) * r, kb[3 * a + b].astype(jnp.float32), g)
            tf[b, ii * ch : (ii + 1) * ch, :] = f.astype(jnp.bfloat16)
            tb[b, ii * ch : (ii + 1) * ch, :] = g.astype(jnp.bfloat16)

    def phase_a(gi, carry):
        side = jnp.where(gi * RG > n // 2, 1, 0)
        for ii in range(RG):
            e = gi * RG + ii
            i = e - MAXDIL
            v8, d8 = validity(e, i, side)
            v = jnp.concatenate([v8] * (ch // RG), axis=0)
            d = jnp.concatenate([d8] * (ch // RG), axis=0)
            rw = rows[e].astype(jnp.float32)
            h = (jnp.concatenate([rw, rw], axis=1) + cols[side]) * v
            h2 = h * h
            t = jnp.tanh(S2PI * h * (1.0 + CUBIC * h2))
            cdf = 0.5 * (1.0 + t)
            act = h * cdf
            dg = cdf + (0.5 * S2PI) * h * (1.0 - t * t) * (1.0 + 3.0 * CUBIC * h2)
            at = pl.ds(pl.multiple_of(e * ch, ch), ch)
            act3[1, at, :] = act.astype(jnp.bfloat16)
            act3[0, at, :] = pltpu.roll(act, r, 1).astype(jnp.bfloat16)
            act3[2, at, :] = pltpu.roll(act, wide - r, 1).astype(jnp.bfloat16)
            ct = jnp.concatenate([cot[e].astype(jnp.float32), halo[e].astype(jnp.float32)], axis=1)
            gz = pltpu.roll(ct, lax.rem(i + wide, wide), 1) * v
            main = (d >= 0) & (d < n)
            gz3[1, at, :] = gz.astype(jnp.bfloat16)
            gz3[2, at, :] = pltpu.roll(gz, r, 1).astype(jnp.bfloat16)
            gz3[0, at, :] = pltpu.roll(gz, wide - r, 1).astype(jnp.bfloat16)
            gzm[at, :] = jnp.where(main, gz, 0.0).astype(jnp.bfloat16)
            hid[at, :] = h
            der[at, :] = jnp.where(main, dg * v, 0.0)
        return carry

    lax.fori_loop(0, groups + 1, phase_a, 0)

    kacc[...] = jnp.zeros_like(kacc)
    bacc[...] = jnp.zeros_like(bacc)
    rsum[...] = jnp.zeros_like(rsum)
    csum[...] = jnp.zeros_like(csum)
    lane_n = lax.broadcasted_iota(jnp.int32, (ch, n), 1)

    def phase_b(gi, carry):
        big = pl.ds(pl.multiple_of(gi * blk, blk), 2 * blk)
        own = pl.ds(pl.multiple_of(gi * blk + MAXDIL * ch, MAXDIL * ch), blk)
        z = jnp.zeros((blk, wide), jnp.float32)
        da = jnp.zeros((blk, wide), jnp.float32)
        g = gzm[own, :]
        for b in range(3):
            x = act3[b, big, :]
            z = z + jnp.dot(tf[b], x, preferred_element_type=jnp.float32)
            da = da + jnp.dot(tb[b], gz3[b, big, :], preferred_element_type=jnp.float32)
            kacc[b] += lax.dot_general(g, x, (((1,), (1,)), ((), ())), preferred_element_type=jnp.float32)
        gf = g.astype(jnp.float32)
        dx = gf + der[own, :] * da
        hz = hid[own, :] + z
        bsum, cs, rs = bacc[...], csum[...], rsum[...]
        for ii in range(RG):
            i = gi * RG + ii
            side = jnp.where(i + MAXDIL >= (n // 2 // RG) * RG + RG, 1, 0)
            v8, _ = validity(i + MAXDIL, i, side)
            v = jnp.concatenate([v8] * (ch // RG), axis=0)
            sl = slice(ii * ch, (ii + 1) * ch)
            po = (hz[sl] + bias[...]) * v
            out[i] = pltpu.roll(po, lax.rem(wide - i, wide), 1)[:, :n].astype(jnp.bfloat16)
            bsum = bsum + gf[sl]
            cs = cs + dx[sl]
            tot = jnp.sum(dx[sl], axis=1, keepdims=True)
            rs = jnp.where(lane_n == i, tot, rs)
        bacc[...] = bsum
        csum[...] = cs
        rsum[...] = rs
        return carry

    lax.fori_loop(0, groups, phase_b, 0)

    lanes = lax.broadcasted_iota(jnp.int32, (RG, 128), 1) // ch
    pieces = []
    for a in range(3):
        for b in range(3):
            s = jnp.zeros((ch, 2 * blk), jnp.float32)
            for ii in range(RG):
                s = s + jnp.where(kblk == ii + MAXDIL + (a - 1) * r, kacc[b, ii * ch : (ii + 1) * ch, :], 0.0)
            f = s[:, :128]
            for m in range(1, 2 * blk // 128):
                f = f + s[:, m * 128 : (m + 1) * 128]
            f = f + pltpu.roll(f, 64, 1)
            f = f + pltpu.roll(f, 32, 1)
            pieces += [f[m * RG : (m + 1) * RG] for m in range(ch // RG)]
    bt = jnp.broadcast_to(jnp.sum(bacc[...], axis=1, keepdims=True), (ch, 128))
    count = len(pieces) // 4
    for s in range(count):
        piece = pieces[s]
        for m in range(1, 4):
            piece = jnp.where(lanes == m, pieces[m * count + s], piece)
        kgrad[s] = piece
    piece = bt[:RG]
    for m in range(1, 4):
        piece = jnp.where(lanes == m, bt[m * RG : (m + 1) * RG], piece)
    kgrad[count] = piece


def sum_kernel(
    R, T, kg, row, col, kg_out, rc_out,
    kbuf, rbuf, abuf, bbuf, ksum, rcsum, kres, rcres,
    ks, kr, rs, rr, as_, ar, bs, br, k2s, k2r, r2s, r2r,
):
    N = R * T
    K, Z = kg.shape[0], row.shape[0]
    q, t = lax.axis_index("row"), lax.axis_index("diag")
    me = q * T + t

    def loop(count, body):
        def step(p, c):
            body(p)
            return c
        lax.fori_loop(0, count, step, 0)

    def send(src, dst, ss, sr, dq, dt):
        return pltpu.make_async_remote_copy(
            src_ref=src, dst_ref=dst, send_sem=ss, recv_sem=sr,
            device_id={"row": dq, "diag": dt}, device_id_type=pl.DeviceIdType.MESH,
        )

    barrier = pltpu.get_barrier_semaphore()

    def greet(p):
        @pl.when(p != me)
        def _():
            pl.semaphore_signal(barrier, inc=1, device_id={"row": p // T, "diag": p % T},
                                device_id_type=pl.DeviceIdType.MESH)
    loop(N, greet)
    pl.semaphore_wait(barrier, N - 1)

    def k1(k):
        return send(kg.at[k], kbuf.at[me], ks.at[k], kr.at[me], k // T, k % T)

    def r1(z):
        return send(row.at[z], rbuf.at[t], rs.at[z], rr.at[t], q, z)

    def a1(z):
        return send(col.at[0, z], abuf.at[q], as_.at[z], ar.at[q], q + t, z)

    def b1(z):
        return send(col.at[1, z], bbuf.at[q], bs.at[z], br.at[q], q + t + 1, z)

    def first(act):
        for k in range(K):
            @pl.when(me != k)
            def _():
                act(k1(k))
        for z in range(Z):
            @pl.when(t != z)
            def _():
                act(r1(z))

            @pl.when((q + t < R) & ((t != 0) | (z != 0)))
            def _():
                act(a1(z))

            @pl.when(q + t + 1 < R)
            def _():
                act(b1(z))

    first(lambda c: c.start())

    def got(buf, sem):
        send(buf, buf, sem, sem, q, t).wait_recv()

    def k2(p):
        return send(ksum, kres.at[me], k2s.at[p], k2r.at[me], p // T, p % T)

    def r2(p):
        return send(rcsum, rcres.at[t], r2s.at[p], r2r.at[t], q, p)

    def second(act):
        @pl.when(me < K)
        def _():
            def one(p):
                @pl.when(p != me)
                def _():
                    act(k2(p))
            loop(N, one)

        @pl.when(t < Z)
        def _():
            def one(p):
                @pl.when(p != t)
                def _():
                    act(r2(p))
            loop(T, one)

    @pl.when(me < K)
    def _():
        ksum[...] = kg[me]

        def take(p):
            @pl.when(p != me)
            def _():
                got(kbuf.at[p], kr.at[p])
                ksum[...] += kbuf[p]
        loop(N, take)
        kres[me] = ksum[...]

    @pl.when(t < Z)
    def _():
        rcsum[0] = row[t]
        rcsum[1] = jnp.zeros_like(rcsum[1])

        def take(p):
            @pl.when(p != t)
            def _():
                got(rbuf.at[p], rr.at[p])
                rcsum[0] += rbuf[p]
        loop(T, take)

        @pl.when(t == 0)
        def _():
            rcsum[1] = col[0, 0]

        def take_col(p):
            @pl.when((p <= q) & (q - p < T) & ((p != q) | (t != 0)))
            def _():
                got(abuf.at[p], ar.at[p])
                rcsum[1] += abuf[p]

            @pl.when((p <= q - 1) & (q - 1 - p < T))
            def _():
                got(bbuf.at[p], br.at[p])
                rcsum[1] += bbuf[p]
        loop(R, take_col)
        rcres[t] = rcsum[...]

    second(lambda c: c.start())
    for k in range(K):
        @pl.when(me != k)
        def _():
            got(kres.at[k], k2r.at[k])
    for z in range(Z):
        @pl.when(t != z)
        def _():
            got(rcres.at[z], r2r.at[z])
    kg_out[...] = kres[...]
    rc_out[...] = rcres[...]
    first(lambda c: c.wait_send())
    second(lambda c: c.wait_send())


def local(emb_rows, emb_cols, kernel, bias, cotangent, valid, dilation, band):
    ch, n = emb_rows.shape
    R, T = lax.axis_size("row"), lax.axis_size("diag")
    q, t = lax.axis_index("row"), lax.axis_index("diag")
    wide, ext, m = 2 * n, n + 2 * MAXDIL, MAXDIL
    bf, f32 = jnp.bfloat16, jnp.float32

    pack = jnp.concatenate(
        [emb_cols, emb_rows, jnp.broadcast_to(valid.astype(bf)[None], (16, n))], axis=0)
    every = lax.all_gather(pack, "row", axis=1, tiled=True)
    every = jnp.pad(every, ((0, 0), (n, n * (T + 2))))
    win = lax.dynamic_slice_in_dim(every, n * (q + t), 4 * n, 1)
    near = lax.dynamic_slice_in_dim(every, n * q, 3 * n, 1)[:, n - m : 2 * n + m]
    s = 28
    low = jnp.concatenate([win[:, n : n + wide - s], win[:, n - s : n]], axis=1)
    high = jnp.concatenate([win[:, n + wide : n + wide + s], win[:, n + s : n + wide]], axis=1)
    both = jnp.stack([low, high]).astype(f32)
    cols = both[:, :ch]
    vcol = both[:, 2 * ch : 2 * ch + RG]
    vr = near[2 * ch].astype(f32)
    rows = jnp.broadcast_to(near[ch : 2 * ch].T[:, :, None], (ext, ch, n))

    cot = jnp.transpose(cotangent, (1, 0, 2))
    before, after = with_halo(cot, "row", 0, m)
    cot = jnp.concatenate([before, cot, after], axis=0)
    before, after = with_halo(cot, "diag", 2, 2 * m)
    halo = jnp.concatenate([after, jnp.zeros((ext, ch, n - 4 * m), bf), before], axis=2)

    blk = RG * ch
    kf = jnp.tile(kernel.reshape(9, ch, ch), (1, 1, 2 * RG))
    kb = jnp.tile(jnp.swapaxes(kernel.reshape(9, ch, ch), 1, 2), (1, 1, 2 * RG))
    par = jnp.stack([dilation[0], band[0], (t * n).astype(jnp.int32)])
    bias2 = jnp.broadcast_to(bias[:, None], (ch, wide))
    nk = (9 * ch * ch) // (RG * 128) + 1
    vmem = pl.BlockSpec(memory_space=pltpu.VMEM)
    smem = pl.BlockSpec(memory_space=pltpu.SMEM)
    out, rsum, csum, kg = pl.pallas_call(
        pair_kernel,
        out_shape=(
            jax.ShapeDtypeStruct((n, ch, n), bf),
            jax.ShapeDtypeStruct((ch, n), f32),
            jax.ShapeDtypeStruct((ch, wide), f32),
            jax.ShapeDtypeStruct((nk, RG, 128), f32),
        ),
        in_specs=[smem, smem] + [vmem] * 8,
        out_specs=(vmem,) * 4,
        scratch_shapes=[
            pltpu.VMEM((3, ext * ch, wide), bf),
            pltpu.VMEM((3, ext * ch, wide), bf),
            pltpu.VMEM((ext * ch, wide), bf),
            pltpu.VMEM((ext * ch, wide), f32),
            pltpu.VMEM((ext * ch, wide), f32),
            pltpu.VMEM((3, blk, 2 * blk), bf),
            pltpu.VMEM((3, blk, 2 * blk), bf),
            pltpu.VMEM((3, blk, 2 * blk), f32),
            pltpu.VMEM((ch, wide), f32),
        ],
        compiler_params=pltpu.CompilerParams(vmem_limit_bytes=56 * 2**20),
        name="pair_kernel",
    )(par, vr, rows, cols, vcol, cot, halo, kf, kb, bias2)

    Z = ch // RG
    dma = pltpu.SemaphoreType.DMA
    tile = lambda *lead: pltpu.VMEM(lead + (RG, n), f32)
    kg, rc = pl.pallas_call(
        functools.partial(sum_kernel, R, T),
        out_shape=(
            jax.ShapeDtypeStruct((nk, RG, 128), f32),
            jax.ShapeDtypeStruct((Z, 2, RG, n), f32),
        ),
        in_specs=[vmem] * 3,
        out_specs=(vmem,) * 2,
        scratch_shapes=[
            tile(R * T), tile(T), tile(R), tile(R), tile(), tile(2), tile(nk), tile(Z, 2),
            dma((nk,)), dma((R * T,)), dma((Z,)), dma((T,)), dma((Z,)), dma((R,)), dma((Z,)), dma((R,)),
            dma((R * T,)), dma((nk,)), dma((T,)), dma((Z,)),
        ],
        compiler_params=pltpu.CompilerParams(collective_id=0, has_side_effects=True),
        name="sum_kernel",
    )(kg, rsum.reshape(Z, RG, n), csum.reshape(Z, RG, 2, n).transpose(2, 0, 1, 3))

    embed_scale = 1.0 / jnp.sqrt(jnp.float32(T * n))
    weight_scale = 1.0 / jnp.sqrt(jnp.float32(R * n) * jnp.float32(T * n))
    kgt = kg[:-1].reshape(-1, 4, ch).transpose(1, 0, 2).reshape(3, 3, ch, ch)
    bgt = kg[-1].reshape(RG, 4, ch)[:, :, 0].T.reshape(ch)
    return (
        jnp.transpose(out, (1, 0, 2)),
        rc[:, 0].reshape(ch, n) * embed_scale,
        rc[:, 1].reshape(ch, n) * embed_scale,
        kgt * weight_scale,
        bgt * weight_scale,
    )


def solution(mesh):
    in_specs = (
        P(None, ("grp", "row")),
        P(None, ("grp", "row")),
        P(),
        P(),
        P(None, ("grp", "row"), "diag"),
        P(("grp", "row")),
        P("grp"),
        P("grp"),
    )
    out_specs = (
        P(None, ("grp", "row"), "diag"),
        P(None, ("grp", "row")),
        P(None, ("grp", "row")),
        P("grp", None, None, None),
        P("grp"),
    )
    return jax.shard_map(local, mesh=mesh, in_specs=in_specs, out_specs=out_specs, check_vma=False)
```

```python
import functools

import jax
import jax.numpy as jnp
from jax import lax
from jax.experimental import pallas as pl
from jax.experimental.pallas import tpu as pltpu
from jax.sharding import PartitionSpec as P

MAXDIL = 4
RG = 8
S2PI = 0.7978845608028654
CUBIC = 0.044715


def loop(count, body):
    def step(p, c):
        body(p)
        return c
    lax.fori_loop(0, count, step, 0)


def send(src, dst, ss, sr, dq, dt):
    return pltpu.make_async_remote_copy(
        src_ref=src, dst_ref=dst, send_sem=ss, recv_sem=sr,
        device_id={"row": dq, "diag": dt}, device_id_type=pl.DeviceIdType.MESH,
    )


def gather_kernel(
    R, T, pack, cot, cols, vcol, near, ext, halo,
    blocks, edge_l, edge_r, from_r, from_l, top, bottom,
    ps, pr, hs, hr,
):
    n, ch = cot.shape[0], cot.shape[1]
    m = MAXDIL
    width = 2 * m
    per = n // width
    tiles = n // per
    q, t = lax.axis_index("row"), lax.axis_index("diag")
    bf, f32 = jnp.bfloat16, jnp.float32
    mesh_id = pl.DeviceIdType.MESH
    barrier = pltpu.get_barrier_semaphore()
    left, right, above, below = t > 0, t < T - 1, q > 0, q < R - 1

    def greet(p):
        @pl.when(p != q)
        def _():
            pl.semaphore_signal(barrier, inc=1, device_id={"row": p, "diag": t}, device_id_type=mesh_id)
    loop(R, greet)
    sides = []
    for dt, okt in ((-1, left), (1, right)):
        for dq, okq in ((-1, above), (0, True), (1, below)):
            sides.append((dq, dt, okt & okq))
    total = R - 1
    for dq, dt, ok in sides:
        total = total + jnp.where(ok, 1, 0)

        @pl.when(ok)
        def _():
            pl.semaphore_signal(barrier, inc=1, device_id={"row": q + dq, "diag": t + dt}, device_id_type=mesh_id)

    lane = lax.broadcasted_iota(jnp.int32, (ch, n), 1)

    def pack_edges(g):
        a = jnp.zeros((ch, n), f32)
        b = jnp.zeros((ch, n), f32)
        for s in range(per):
            x = cot[g * per + s].astype(f32)
            here = lane // width == s
            a = jnp.where(here, pltpu.roll(x, width * s, 1) if s else x, a)
            sh = (width * (s + 1)) % n
            b = jnp.where(here, pltpu.roll(x, sh, 1) if sh else x, b)
        edge_l[g] = a.astype(bf)
        edge_r[g] = b.astype(bf)
    loop(tiles, pack_edges)
    pl.semaphore_wait(barrier, total)

    def p1(p):
        return send(pack, blocks.at[q + 1], ps.at[p], pr.at[q], p, t)

    def halos(act):
        last = tiles - 1
        plan = (
            (left, edge_l, from_r.at[pl.ds(0, tiles)], 0, 0, -1),
            (right, edge_r, from_l.at[pl.ds(0, tiles)], 1, 0, 1),
            (above, cot.at[pl.ds(0, m)], bottom, 2, -1, 0),
            (below, cot.at[pl.ds(n - m, m)], top, 3, 1, 0),
            (below & left, edge_l.at[last], from_r.at[tiles], 4, 1, -1),
            (above & left, edge_l.at[0], from_r.at[tiles + 1], 5, -1, -1),
            (below & right, edge_r.at[last], from_l.at[tiles], 6, 1, 1),
            (above & right, edge_r.at[0], from_l.at[tiles + 1], 7, -1, 1),
        )
        flags = {(0, -1): right, (0, 1): left, (-1, 0): below, (1, 0): above,
                 (1, -1): above & right, (-1, -1): below & right, (1, 1): above & left, (-1, 1): below & left}
        for ok, src, dst, k, dq, dt in plan:
            act(ok, flags[(dq, dt)], src, dst, send(src, dst, hs.at[k], hr.at[k], q + dq, t + dt))

    def start(ok, got, src, dst, c):
        @pl.when(ok)
        def _():
            c.start()

    def peers(act):
        def one(p):
            @pl.when(p != q)
            def _():
                act(p)
        loop(R, one)

    peers(lambda p: p1(p).start())
    halos(start)

    zero = jnp.zeros(pack.shape, bf)
    blocks[0] = zero
    for k in range(R + 1, R + T + 3):
        blocks[k] = zero
    blocks[q + 1] = pack[...]

    def body_copy(g):
        for s in range(RG):
            ext[m + g * RG + s] = cot[g * RG + s]
    loop(n // RG, body_copy)

    peers(lambda p: send(pack, blocks.at[p + 1], ps.at[p], pr.at[p], q, t).wait_recv())
    rows_of = slice(ch, 2 * ch + RG)
    lane2 = lax.broadcasted_iota(jnp.int32, pack.shape, 1)
    b0, b1, b2, b3 = (blocks[q + t + k].astype(f32) for k in range(4))
    s = 28
    low = (b1, jnp.where(lane2 >= n - s, b0, b2))
    high = (jnp.where(lane2 < s, b3, b1), b2)
    for side, (x, y) in enumerate((low, high)):
        cols[side, :, :n] = x[:ch]
        cols[side, :, n:] = y[:ch]
        vcol[side, :, :n] = x[2 * ch : 2 * ch + RG]
        vcol[side, :, n:] = y[2 * ch : 2 * ch + RG]
    near[0] = blocks[q + 1].astype(f32)[rows_of]
    near[1] = jnp.where(lane2 >= n - m, blocks[q].astype(f32), blocks[q + 2].astype(f32))[rows_of]

    def finish(ok, got, src, dst, c):
        @pl.when(got)
        def _():
            c.wait_recv()

        @pl.when(jnp.logical_not(got))
        def _():
            dst[...] = jnp.zeros(dst.shape, bf)
    halos(finish)
    for s in range(m):
        ext[s] = top[s]
        ext[n + m + s] = bottom[s]

    def spread(e, tile_r, tile_l, s):
        a = pltpu.roll(tile_r, (n - width * s) % n, 1) if s else tile_r
        b = pltpu.roll(tile_l, (2 * n - width - width * s) % n, 1) if (n - width - width * s) % n else tile_l
        halo[e] = jnp.where(lane < width, a, jnp.where(lane >= n - width, b, 0.0)).astype(bf)

    def unpack(g):
        tr, tl = from_r[g].astype(f32), from_l[g].astype(f32)
        for s in range(per):
            spread(m + g * per + s, tr, tl, s)
    loop(tiles, unpack)
    tr, tl = from_r[tiles].astype(f32), from_l[tiles].astype(f32)
    for s in range(m):
        spread(s, tr, tl, per - m + s)
    tr, tl = from_r[tiles + 1].astype(f32), from_l[tiles + 1].astype(f32)
    for s in range(m):
        spread(n + m + s, tr, tl, s)

    peers(lambda p: p1(p).wait_send())

    def sent(ok, got, src, dst, c):
        @pl.when(ok)
        def _():
            c.wait_send()
    halos(sent)


def pair_kernel(
    dilation, band, near, cols, vcol, cot, halo, kf, kb, bias,
    out, rout, cout, kgrad,
    act3, gz3, gzm, hid, der, tf, tb, kacc, bacc, rsum, csum,
):
    n = out.shape[0]
    ch = out.shape[1]
    wide = 2 * n
    r, w, d0 = dilation[0], band[0], lax.axis_index("diag") * n
    groups = n // RG
    blk = RG * ch
    lane1 = lax.broadcasted_iota(jnp.int32, (RG, wide), 1)

    def offsets(i):
        d = lane1 - i
        d = jnp.where(d < -(n // 2), d + wide, d)
        return jnp.where(d >= wide - n // 2, d - wide, d)

    def at_row(i, first, size):
        half = jnp.where((i < 0) | (i >= n), 1, 0)
        x = pltpu.roll(near[half, first : first + size, :], lax.rem(2 * n - i, n), 1)
        return jnp.broadcast_to(x[:, :1], (size, wide))

    def validity(i, side):
        d = offsets(i)
        inside = (d + d0 >= 0) & (d + d0 < w)
        v = jnp.where(inside, vcol[side] * at_row(i, ch, RG), 0.0)
        return v, d

    reps = 2 * blk // kf.shape[2]
    kblk = lax.broadcasted_iota(jnp.int32, (ch, 2 * blk), 1) // ch
    for b in range(3):
        for ii in range(RG):
            f = jnp.zeros((ch, 2 * blk), jnp.float32)
            g = jnp.zeros((ch, 2 * blk), jnp.float32)
            for a in range(3):
                f = jnp.where(kblk == ii + MAXDIL + (a - 1) * r, jnp.concatenate([kf[3 * a + b].astype(jnp.float32)] * reps, axis=1), f)
                g = jnp.where(kblk == ii + MAXDIL - (a - 1) * r, jnp.concatenate([kb[3 * a + b].astype(jnp.float32)] * reps, axis=1), g)
            tf[b, ii * ch : (ii + 1) * ch, :] = f.astype(jnp.bfloat16)
            tb[b, ii * ch : (ii + 1) * ch, :] = g.astype(jnp.bfloat16)

    def phase_a(gi, carry):
        side = jnp.where(gi * RG > n // 2, 1, 0)
        for ii in range(RG):
            e = gi * RG + ii
            i = e - MAXDIL
            v8, d8 = validity(i, side)
            v = jnp.concatenate([v8] * (ch // RG), axis=0)
            d = jnp.concatenate([d8] * (ch // RG), axis=0)
            h = (at_row(i, 0, ch) + cols[side]) * v
            h2 = h * h
            t = jnp.tanh(S2PI * h * (1.0 + CUBIC * h2))
            cdf = 0.5 * (1.0 + t)
            act = h * cdf
            dg = cdf + (0.5 * S2PI) * h * (1.0 - t * t) * (1.0 + 3.0 * CUBIC * h2)
            at = pl.ds(pl.multiple_of(e * ch, ch), ch)
            act3[1, at, :] = act.astype(jnp.bfloat16)
            act3[0, at, :] = pltpu.roll(act, r, 1).astype(jnp.bfloat16)
            act3[2, at, :] = pltpu.roll(act, wide - r, 1).astype(jnp.bfloat16)
            ct = jnp.concatenate([cot[e].astype(jnp.float32), halo[e].astype(jnp.float32)], axis=1)
            gz = pltpu.roll(ct, lax.rem(i + wide, wide), 1) * v
            main = (d >= 0) & (d < n)
            gz3[1, at, :] = gz.astype(jnp.bfloat16)
            gz3[2, at, :] = pltpu.roll(gz, r, 1).astype(jnp.bfloat16)
            gz3[0, at, :] = pltpu.roll(gz, wide - r, 1).astype(jnp.bfloat16)
            gzm[at, :] = jnp.where(main, gz, 0.0).astype(jnp.bfloat16)
            hid[at, :] = h
            der[at, :] = jnp.where(main, dg * v, 0.0)
        return carry

    lax.fori_loop(0, groups + 1, phase_a, 0)

    kacc[...] = jnp.zeros_like(kacc)
    bacc[...] = jnp.zeros_like(bacc)
    rsum[...] = jnp.zeros_like(rsum)
    csum[...] = jnp.zeros_like(csum)
    lane_n = lax.broadcasted_iota(jnp.int32, (ch, n), 1)

    def phase_b(gi, carry):
        big = pl.ds(pl.multiple_of(gi * blk, blk), 2 * blk)
        own = pl.ds(pl.multiple_of(gi * blk + MAXDIL * ch, MAXDIL * ch), blk)
        z = jnp.zeros((blk, wide), jnp.float32)
        da = jnp.zeros((blk, wide), jnp.float32)
        g = gzm[own, :]
        for b in range(3):
            x = act3[b, big, :]
            z = z + jnp.dot(tf[b], x, preferred_element_type=jnp.float32)
            da = da + jnp.dot(tb[b], gz3[b, big, :], preferred_element_type=jnp.float32)
            kacc[b] += lax.dot_general(g, x, (((1,), (1,)), ((), ())), preferred_element_type=jnp.float32)
        gf = g.astype(jnp.float32)
        dx = gf + der[own, :] * da
        hz = hid[own, :] + z
        bsum, cs, rs = bacc[...], csum[...], rsum[...]
        for ii in range(RG):
            i = gi * RG + ii
            side = jnp.where(i + MAXDIL >= (n // 2 // RG) * RG + RG, 1, 0)
            v8, _ = validity(i, side)
            v = jnp.concatenate([v8] * (ch // RG), axis=0)
            sl = slice(ii * ch, (ii + 1) * ch)
            po = (hz[sl] + bias[...]) * v
            out[i] = pltpu.roll(po, lax.rem(wide - i, wide), 1)[:, :n].astype(jnp.bfloat16)
            bsum = bsum + gf[sl]
            cs = cs + dx[sl]
            tot = jnp.sum(dx[sl], axis=1, keepdims=True)
            rs = jnp.where(lane_n == i, tot, rs)
        bacc[...] = bsum
        csum[...] = cs
        rsum[...] = rs
        return carry

    lax.fori_loop(0, groups, phase_b, 0)

    for z in range(ch // RG):
        rout[z] = rsum[z * RG : (z + 1) * RG, :]
        for k in range(2):
            cout[k, z] = csum[z * RG : (z + 1) * RG, k * n : (k + 1) * n]
    lanes = lax.broadcasted_iota(jnp.int32, (RG, 128), 1) // ch
    pieces = []
    for a in range(3):
        for b in range(3):
            s = jnp.zeros((ch, 2 * blk), jnp.float32)
            for ii in range(RG):
                s = s + jnp.where(kblk == ii + MAXDIL + (a - 1) * r, kacc[b, ii * ch : (ii + 1) * ch, :], 0.0)
            f = s[:, :128]
            for m in range(1, 2 * blk // 128):
                f = f + s[:, m * 128 : (m + 1) * 128]
            f = f + pltpu.roll(f, 64, 1)
            f = f + pltpu.roll(f, 32, 1)
            pieces += [f[m * RG : (m + 1) * RG] for m in range(ch // RG)]
    bt = jnp.broadcast_to(jnp.sum(bacc[...], axis=1, keepdims=True), (ch, 128))
    count = len(pieces) // 4
    for s in range(count):
        piece = pieces[s]
        for m in range(1, 4):
            piece = jnp.where(lanes == m, pieces[m * count + s], piece)
        kgrad[s] = piece
    piece = bt[:RG]
    for m in range(1, 4):
        piece = jnp.where(lanes == m, bt[m * RG : (m + 1) * RG], piece)
    kgrad[count] = piece


def sum_kernel(
    R, T, embed_scale, weight_scale, kg, row, col, kg_out, row_out, col_out,
    kbuf, rbuf, abuf, bbuf, ksum, rcsum, kres, rcres,
    ks, kr, rs, rr, as_, ar, bs, br, k2s, k2r, r2s, r2r,
):
    N = R * T
    K, Z = kg.shape[0], row.shape[0]
    q, t = lax.axis_index("row"), lax.axis_index("diag")
    me = q * T + t

    barrier = pltpu.get_barrier_semaphore()

    def greet(p):
        @pl.when(p != me)
        def _():
            pl.semaphore_signal(barrier, inc=1, device_id={"row": p // T, "diag": p % T},
                                device_id_type=pl.DeviceIdType.MESH)
    loop(N, greet)
    pl.semaphore_wait(barrier, N - 1)

    def k1(k):
        return send(kg.at[k], kbuf.at[me], ks.at[k], kr.at[me], k // T, k % T)

    def r1(z):
        return send(row.at[z], rbuf.at[t], rs.at[z], rr.at[t], q, z)

    def a1(z):
        return send(col.at[0, z], abuf.at[q], as_.at[z], ar.at[q], q + t, z)

    def b1(z):
        return send(col.at[1, z], bbuf.at[q], bs.at[z], br.at[q], q + t + 1, z)

    def first(act):
        for k in range(K):
            @pl.when(me != k)
            def _():
                act(k1(k))
        for z in range(Z):
            @pl.when(t != z)
            def _():
                act(r1(z))

            @pl.when((q + t < R) & ((t != 0) | (z != 0)))
            def _():
                act(a1(z))

            @pl.when(q + t + 1 < R)
            def _():
                act(b1(z))

    first(lambda c: c.start())

    def got(buf, sem):
        send(buf, buf, sem, sem, q, t).wait_recv()

    def k2(p):
        return send(ksum, kres.at[me], k2s.at[p], k2r.at[me], p // T, p % T)

    def r2(p):
        return send(rcsum, rcres.at[t], r2s.at[p], r2r.at[t], q, p)

    def second(act):
        @pl.when(me < K)
        def _():
            def one(p):
                @pl.when(p != me)
                def _():
                    act(k2(p))
            loop(N, one)

        @pl.when(t < Z)
        def _():
            def one(p):
                @pl.when(p != t)
                def _():
                    act(r2(p))
            loop(T, one)

    @pl.when(me < K)
    def _():
        ksum[...] = kg[me]

        def take(p):
            @pl.when(p != me)
            def _():
                got(kbuf.at[p], kr.at[p])
                ksum[...] += kbuf[p]
        loop(N, take)
        ksum[...] = ksum[...] * weight_scale
        kres[me] = ksum[...]

    @pl.when(t < Z)
    def _():
        rcsum[0] = row[t]
        rcsum[1] = jnp.zeros_like(rcsum[1])

        def take(p):
            @pl.when(p != t)
            def _():
                got(rbuf.at[p], rr.at[p])
                rcsum[0] += rbuf[p]
        loop(T, take)

        @pl.when(t == 0)
        def _():
            rcsum[1] = col[0, 0]

        def take_col(p):
            @pl.when((p <= q) & (q - p < T) & ((p != q) | (t != 0)))
            def _():
                got(abuf.at[p], ar.at[p])
                rcsum[1] += abuf[p]

            @pl.when((p <= q - 1) & (q - 1 - p < T))
            def _():
                got(bbuf.at[p], br.at[p])
                rcsum[1] += bbuf[p]
        loop(R, take_col)
        rcsum[...] = rcsum[...] * embed_scale
        rcres[t] = rcsum[...]

    second(lambda c: c.start())
    for k in range(K):
        @pl.when(me != k)
        def _():
            got(kres.at[k], k2r.at[k])
    for z in range(Z):
        @pl.when(t != z)
        def _():
            got(rcres.at[z], r2r.at[z])
    kg_out[...] = kres[...]
    for z in range(Z):
        row_out[z * RG : (z + 1) * RG, :] = rcres[z, 0]
        col_out[z * RG : (z + 1) * RG, :] = rcres[z, 1]
    first(lambda c: c.wait_send())
    second(lambda c: c.wait_send())


def local(emb_rows, emb_cols, kernel, bias, cotangent, valid, dilation, band):
    ch, n = emb_rows.shape
    R, T = lax.axis_size("row"), lax.axis_size("diag")
    wide, ext, m = 2 * n, n + 2 * MAXDIL, MAXDIL
    bf, f32 = jnp.bfloat16, jnp.float32

    pack = jnp.concatenate(
        [emb_cols, emb_rows, jnp.broadcast_to(valid.astype(bf)[None], (16, n))], axis=0)
    cot = jnp.transpose(cotangent, (1, 0, 2))
    vmem = pl.BlockSpec(memory_space=pltpu.VMEM)
    smem = pl.BlockSpec(memory_space=pltpu.SMEM)
    dma = pltpu.SemaphoreType.DMA
    tiles = 2 * m
    edges = lambda k: pltpu.VMEM((k, ch, n), bf)
    cols, vcol, near, cot, halo = pl.pallas_call(
        functools.partial(gather_kernel, R, T),
        out_shape=(
            jax.ShapeDtypeStruct((2, ch, wide), f32),
            jax.ShapeDtypeStruct((2, RG, wide), f32),
            jax.ShapeDtypeStruct((2, ch + RG, n), f32),
            jax.ShapeDtypeStruct((ext, ch, n), bf),
            jax.ShapeDtypeStruct((ext, ch, n), bf),
        ),
        in_specs=[vmem] * 2,
        out_specs=(vmem,) * 5,
        scratch_shapes=[
            pltpu.VMEM((R + T + 3,) + pack.shape, bf),
            edges(tiles), edges(tiles), edges(tiles + 2), edges(tiles + 2), edges(m), edges(m),
            dma((R,)), dma((R,)), dma((8,)), dma((8,)),
        ],
        compiler_params=pltpu.CompilerParams(collective_id=1, has_side_effects=True),
        name="gather_kernel",
    )(pack, cot)

    blk = RG * ch
    kf = jnp.tile(kernel.reshape(9, ch, ch), (1, 1, 4))
    kb = jnp.tile(jnp.swapaxes(kernel.reshape(9, ch, ch), 1, 2), (1, 1, 4))
    bias2 = jnp.broadcast_to(bias[:, None], (ch, wide))
    nk = (9 * ch * ch) // (RG * 128) + 1
    Z = ch // RG
    out, rsum, csum, kg = pl.pallas_call(
        pair_kernel,
        out_shape=(
            jax.ShapeDtypeStruct((n, ch, n), bf),
            jax.ShapeDtypeStruct((Z, RG, n), f32),
            jax.ShapeDtypeStruct((2, Z, RG, n), f32),
            jax.ShapeDtypeStruct((nk, RG, 128), f32),
        ),
        in_specs=[smem, smem] + [vmem] * 8,
        out_specs=(vmem,) * 4,
        scratch_shapes=[
            pltpu.VMEM((3, ext * ch, wide), bf),
            pltpu.VMEM((3, ext * ch, wide), bf),
            pltpu.VMEM((ext * ch, wide), bf),
            pltpu.VMEM((ext * ch, wide), f32),
            pltpu.VMEM((ext * ch, wide), f32),
            pltpu.VMEM((3, blk, 2 * blk), bf),
            pltpu.VMEM((3, blk, 2 * blk), bf),
            pltpu.VMEM((3, blk, 2 * blk), f32),
            pltpu.VMEM((ch, wide), f32),
            pltpu.VMEM((ch, n), f32),
            pltpu.VMEM((ch, wide), f32),
        ],
        compiler_params=pltpu.CompilerParams(vmem_limit_bytes=56 * 2**20),
        name="pair_kernel",
    )(dilation, band, near, cols, vcol, cot, halo, kf, kb, bias2)

    tile = lambda *lead: pltpu.VMEM(lead + (RG, n), f32)
    embed_scale = float(T * n) ** -0.5
    weight_scale = float(R * n * T * n) ** -0.5
    kg, row_grad, col_grad = pl.pallas_call(
        functools.partial(sum_kernel, R, T, embed_scale, weight_scale),
        out_shape=(
            jax.ShapeDtypeStruct((nk, RG, 128), f32),
            jax.ShapeDtypeStruct((ch, n), f32),
            jax.ShapeDtypeStruct((ch, n), f32),
        ),
        in_specs=[vmem] * 3,
        out_specs=(vmem,) * 3,
        scratch_shapes=[
            tile(R * T), tile(T), tile(R), tile(R), tile(), tile(2), tile(nk), tile(Z, 2),
            dma((nk,)), dma((R * T,)), dma((Z,)), dma((T,)), dma((Z,)), dma((R,)), dma((Z,)), dma((R,)),
            dma((R * T,)), dma((nk,)), dma((T,)), dma((Z,)),
        ],
        compiler_params=pltpu.CompilerParams(collective_id=0, has_side_effects=True),
        name="sum_kernel",
    )(kg, rsum, csum)

    kgt = kg[:-1].reshape(-1, 4, ch).transpose(1, 0, 2).reshape(3, 3, ch, ch)
    bgt = kg[-1].reshape(RG, 4, ch)[:, :, 0].T.reshape(ch)
    return (
        jnp.transpose(out, (1, 0, 2)),
        row_grad,
        col_grad,
        kgt,
        bgt,
    )


def solution(mesh):
    in_specs = (
        P(None, ("grp", "row")),
        P(None, ("grp", "row")),
        P(),
        P(),
        P(None, ("grp", "row"), "diag"),
        P(("grp", "row")),
        P("grp"),
        P("grp"),
    )
    out_specs = (
        P(None, ("grp", "row"), "diag"),
        P(None, ("grp", "row")),
        P(None, ("grp", "row")),
        P("grp", None, None, None),
        P("grp"),
    )
    return jax.shard_map(local, mesh=mesh, in_specs=in_specs, out_specs=out_specs, check_vma=False)
```

```python
import functools

import jax
import jax.numpy as jnp
from jax import lax
from jax.experimental import pallas as pl
from jax.experimental.pallas import tpu as pltpu
from jax.sharding import PartitionSpec as P

MAXDIL = 4
RG = 8
S2PI = 0.7978845608028654
CUBIC = 0.044715


def loop(count, body):
    def step(p, c):
        body(p)
        return c
    lax.fori_loop(0, count, step, 0)


def send(src, dst, ss, sr, dq, dt):
    return pltpu.make_async_remote_copy(
        src_ref=src, dst_ref=dst, send_sem=ss, recv_sem=sr,
        device_id={"row": dq, "diag": dt}, device_id_type=pl.DeviceIdType.MESH,
    )


def gather_kernel(
    R, T, pack, cot, cols, vcol, near, ext, halo,
    blocks, edge_l, edge_r, from_r, from_l, top, bottom,
    ps, pr, hs, hr,
):
    n, ch = cot.shape[0], cot.shape[1]
    m = MAXDIL
    width = 2 * m
    per = n // width
    tiles = n // per
    q, t = lax.axis_index("row"), lax.axis_index("diag")
    bf, f32 = jnp.bfloat16, jnp.float32
    mesh_id = pl.DeviceIdType.MESH
    barrier = pltpu.get_barrier_semaphore()
    left, right, above, below = t > 0, t < T - 1, q > 0, q < R - 1

    def greet(p):
        @pl.when(p != q)
        def _():
            pl.semaphore_signal(barrier, inc=1, device_id={"row": p, "diag": t}, device_id_type=mesh_id)
    loop(R, greet)
    sides = []
    for dt, okt in ((-1, left), (1, right)):
        for dq, okq in ((-1, above), (0, True), (1, below)):
            sides.append((dq, dt, okt & okq))
    total = R - 1
    for dq, dt, ok in sides:
        total = total + jnp.where(ok, 1, 0)

        @pl.when(ok)
        def _():
            pl.semaphore_signal(barrier, inc=1, device_id={"row": q + dq, "diag": t + dt}, device_id_type=mesh_id)

    lane = lax.broadcasted_iota(jnp.int32, (ch, n), 1)

    def pack_edges(g):
        a = jnp.zeros((ch, n), f32)
        b = jnp.zeros((ch, n), f32)
        for s in range(per):
            x = cot[g * per + s].astype(f32)
            here = lane // width == s
            a = jnp.where(here, pltpu.roll(x, width * s, 1) if s else x, a)
            sh = (width * (s + 1)) % n
            b = jnp.where(here, pltpu.roll(x, sh, 1) if sh else x, b)
        edge_l[g] = a.astype(bf)
        edge_r[g] = b.astype(bf)
    loop(tiles, pack_edges)
    pl.semaphore_wait(barrier, total)

    def p1(p):
        return send(pack, blocks.at[q + 1], ps.at[p], pr.at[q], p, t)

    def halos(act):
        last = tiles - 1
        plan = (
            (left, edge_l, from_r.at[pl.ds(0, tiles)], 0, 0, -1),
            (right, edge_r, from_l.at[pl.ds(0, tiles)], 1, 0, 1),
            (above, cot.at[pl.ds(0, m)], bottom, 2, -1, 0),
            (below, cot.at[pl.ds(n - m, m)], top, 3, 1, 0),
            (below & left, edge_l.at[last], from_r.at[tiles], 4, 1, -1),
            (above & left, edge_l.at[0], from_r.at[tiles + 1], 5, -1, -1),
            (below & right, edge_r.at[last], from_l.at[tiles], 6, 1, 1),
            (above & right, edge_r.at[0], from_l.at[tiles + 1], 7, -1, 1),
        )
        flags = {(0, -1): right, (0, 1): left, (-1, 0): below, (1, 0): above,
                 (1, -1): above & right, (-1, -1): below & right, (1, 1): above & left, (-1, 1): below & left}
        for ok, src, dst, k, dq, dt in plan:
            act(ok, flags[(dq, dt)], src, dst, send(src, dst, hs.at[k], hr.at[k], q + dq, t + dt))

    def start(ok, got, src, dst, c):
        @pl.when(ok)
        def _():
            c.start()

    def peers(act):
        def one(p):
            @pl.when(p != q)
            def _():
                act(p)
        loop(R, one)

    peers(lambda p: p1(p).start())
    halos(start)

    zero = jnp.zeros(pack.shape, bf)
    blocks[0] = zero
    for k in range(R + 1, R + T + 3):
        blocks[k] = zero
    blocks[q + 1] = pack[...]

    def body_copy(g):
        for s in range(RG):
            ext[m + g * RG + s] = cot[g * RG + s]
    loop(n // RG, body_copy)

    peers(lambda p: send(pack, blocks.at[p + 1], ps.at[p], pr.at[p], q, t).wait_recv())
    rows_of = slice(ch, 2 * ch + RG)
    lane2 = lax.broadcasted_iota(jnp.int32, pack.shape, 1)
    b0, b1, b2, b3 = (blocks[q + t + k].astype(f32) for k in range(4))
    s = 28
    low = (b1, jnp.where(lane2 >= n - s, b0, b2))
    high = (jnp.where(lane2 < s, b3, b1), b2)
    for side, (x, y) in enumerate((low, high)):
        cols[side, :, :n] = x[:ch]
        cols[side, :, n:] = y[:ch]
        vcol[side, :, :n] = x[2 * ch : 2 * ch + RG]
        vcol[side, :, n:] = y[2 * ch : 2 * ch + RG]
    near[0] = blocks[q + 1].astype(f32)[rows_of]
    near[1] = jnp.where(lane2 >= n - m, blocks[q].astype(f32), blocks[q + 2].astype(f32))[rows_of]

    def finish(ok, got, src, dst, c):
        @pl.when(got)
        def _():
            c.wait_recv()

        @pl.when(jnp.logical_not(got))
        def _():
            dst[...] = jnp.zeros(dst.shape, bf)
    halos(finish)
    for s in range(m):
        ext[s] = top[s]
        ext[n + m + s] = bottom[s]

    def spread(e, tile_r, tile_l, s):
        a = pltpu.roll(tile_r, (n - width * s) % n, 1) if s else tile_r
        b = pltpu.roll(tile_l, (2 * n - width - width * s) % n, 1) if (n - width - width * s) % n else tile_l
        halo[e] = jnp.where(lane < width, a, jnp.where(lane >= n - width, b, 0.0)).astype(bf)

    def unpack(g):
        tr, tl = from_r[g].astype(f32), from_l[g].astype(f32)
        for s in range(per):
            spread(m + g * per + s, tr, tl, s)
    loop(tiles, unpack)
    tr, tl = from_r[tiles].astype(f32), from_l[tiles].astype(f32)
    for s in range(m):
        spread(s, tr, tl, per - m + s)
    tr, tl = from_r[tiles + 1].astype(f32), from_l[tiles + 1].astype(f32)
    for s in range(m):
        spread(n + m + s, tr, tl, s)

    peers(lambda p: p1(p).wait_send())

    def sent(ok, got, src, dst, c):
        @pl.when(ok)
        def _():
            c.wait_send()
    halos(sent)


def pair_kernel(
    dilation, band, near, cols, vcol, cot, halo, kf, bias,
    out, rout, cout, kgrad,
    act3, gz3, gzm, hid, der, tf, tb, kacc, bacc, rsum, csum, vbuf,
):
    n = out.shape[0]
    ch = out.shape[1]
    wide = 2 * n
    r, w, d0 = dilation[0], band[0], lax.axis_index("diag") * n
    groups = n // RG
    blk = RG * ch
    lane1 = lax.broadcasted_iota(jnp.int32, (RG, wide), 1)

    def offsets(i):
        d = lane1 - i
        d = jnp.where(d < -(n // 2), d + wide, d)
        return jnp.where(d >= wide - n // 2, d - wide, d)

    def at_row(i, first, size):
        half = jnp.where((i < 0) | (i >= n), 1, 0)
        x = pltpu.roll(near[half, first : first + size, :], lax.rem(2 * n - i, n), 1)
        return jnp.broadcast_to(x[:, :1], (size, wide))

    def validity(i, side):
        d = offsets(i)
        inside = (d + d0 >= 0) & (d + d0 < w)
        v = jnp.where(inside, vcol[side] * at_row(i, ch, RG), 0.0)
        return v, d

    def tiled(x):
        return jnp.concatenate([jnp.concatenate([x] * 4, axis=1)] * (2 * blk // (4 * ch)), axis=1)

    kblk = lax.broadcasted_iota(jnp.int32, (ch, 2 * blk), 1) // ch
    for b in range(3):
        fw = [tiled(kf[3 * a + b].astype(jnp.float32)) for a in range(3)]
        bw = [tiled(kf[3 * a + b].astype(jnp.float32).T) for a in range(3)]
        for ii in range(RG):
            f = jnp.zeros((ch, 2 * blk), jnp.float32)
            g = jnp.zeros((ch, 2 * blk), jnp.float32)
            for a in range(3):
                f = jnp.where(kblk == ii + MAXDIL + (a - 1) * r, fw[a], f)
                g = jnp.where(kblk == ii + MAXDIL - (a - 1) * r, bw[a], g)
            tf[b, ii * ch : (ii + 1) * ch, :] = f.astype(jnp.bfloat16)
            tb[b, ii * ch : (ii + 1) * ch, :] = g.astype(jnp.bfloat16)

    def phase_a(gi, carry):
        side = jnp.where(gi * RG > n // 2, 1, 0)
        for ii in range(RG):
            e = gi * RG + ii
            i = e - MAXDIL
            v8, d8 = validity(i, side)
            vbuf[e] = v8
            v = jnp.concatenate([v8] * (ch // RG), axis=0)
            d = jnp.concatenate([d8] * (ch // RG), axis=0)
            h = (at_row(i, 0, ch) + cols[side]) * v
            h2 = h * h
            t = jnp.tanh(S2PI * h * (1.0 + CUBIC * h2))
            cdf = 0.5 * (1.0 + t)
            act = h * cdf
            dg = cdf + (0.5 * S2PI) * h * (1.0 - t * t) * (1.0 + 3.0 * CUBIC * h2)
            at = pl.ds(pl.multiple_of(e * ch, ch), ch)
            act3[1, at, :] = act.astype(jnp.bfloat16)
            act3[0, at, :] = pltpu.roll(act, r, 1).astype(jnp.bfloat16)
            act3[2, at, :] = pltpu.roll(act, wide - r, 1).astype(jnp.bfloat16)
            ct = jnp.concatenate([cot[e].astype(jnp.float32), halo[e].astype(jnp.float32)], axis=1)
            gz = pltpu.roll(ct, lax.rem(i + wide, wide), 1) * v
            main = (d >= 0) & (d < n)
            gz3[1, at, :] = gz.astype(jnp.bfloat16)
            gz3[2, at, :] = pltpu.roll(gz, r, 1).astype(jnp.bfloat16)
            gz3[0, at, :] = pltpu.roll(gz, wide - r, 1).astype(jnp.bfloat16)
            gzm[at, :] = jnp.where(main, gz, 0.0).astype(jnp.bfloat16)
            hid[at, :] = h
            der[at, :] = jnp.where(main, dg * v, 0.0)
        return carry

    lax.fori_loop(0, groups + 1, phase_a, 0)

    kacc[...] = jnp.zeros_like(kacc)
    bacc[...] = jnp.zeros_like(bacc)
    rsum[...] = jnp.zeros_like(rsum)
    csum[...] = jnp.zeros_like(csum)
    lane_n = lax.broadcasted_iota(jnp.int32, (ch, n), 1)

    bias_all = jnp.broadcast_to(bias[...], (ch, wide))

    def phase_b(gi, carry):
        big = pl.ds(pl.multiple_of(gi * blk, blk), 2 * blk)
        own = pl.ds(pl.multiple_of(gi * blk + MAXDIL * ch, MAXDIL * ch), blk)
        z = jnp.zeros((blk, wide), jnp.float32)
        da = jnp.zeros((blk, wide), jnp.float32)
        g = gzm[own, :]
        for b in range(3):
            x = act3[b, big, :]
            z = z + jnp.dot(tf[b], x, preferred_element_type=jnp.float32)
            da = da + jnp.dot(tb[b], gz3[b, big, :], preferred_element_type=jnp.float32)
            kacc[b] += lax.dot_general(g, x, (((1,), (1,)), ((), ())), preferred_element_type=jnp.float32)
        gf = g.astype(jnp.float32)
        dx = gf + der[own, :] * da
        hz = hid[own, :] + z
        bsum, cs, rs = bacc[...], csum[...], rsum[...]
        for ii in range(RG):
            i = gi * RG + ii
            v = jnp.concatenate([vbuf[i + MAXDIL]] * (ch // RG), axis=0)
            sl = slice(ii * ch, (ii + 1) * ch)
            po = (hz[sl] + bias_all) * v
            out[i] = pltpu.roll(po, lax.rem(wide - i, wide), 1)[:, :n].astype(jnp.bfloat16)
            bsum = bsum + gf[sl]
            cs = cs + dx[sl]
            tot = jnp.sum(dx[sl], axis=1, keepdims=True)
            rs = jnp.where(lane_n == i, tot, rs)
        bacc[...] = bsum
        csum[...] = cs
        rsum[...] = rs
        return carry

    lax.fori_loop(0, groups, phase_b, 0)

    for z in range(ch // RG):
        rout[z] = rsum[z * RG : (z + 1) * RG, :]
        for k in range(2):
            cout[k, z] = csum[z * RG : (z + 1) * RG, k * n : (k + 1) * n]
    lanes = lax.broadcasted_iota(jnp.int32, (RG, 128), 1) // ch
    pieces = []
    for a in range(3):
        for b in range(3):
            s = jnp.zeros((ch, 2 * blk), jnp.float32)
            for ii in range(RG):
                s = s + jnp.where(kblk == ii + MAXDIL + (a - 1) * r, kacc[b, ii * ch : (ii + 1) * ch, :], 0.0)
            f = s[:, :128]
            for m in range(1, 2 * blk // 128):
                f = f + s[:, m * 128 : (m + 1) * 128]
            f = f + pltpu.roll(f, 64, 1)
            f = f + pltpu.roll(f, 32, 1)
            pieces += [f[m * RG : (m + 1) * RG] for m in range(ch // RG)]
    bt = jnp.broadcast_to(jnp.sum(bacc[...], axis=1, keepdims=True), (ch, 128))
    count = len(pieces) // 4
    for s in range(count):
        piece = pieces[s]
        for m in range(1, 4):
            piece = jnp.where(lanes == m, pieces[m * count + s], piece)
        kgrad[s] = piece
    piece = bt[:RG]
    for m in range(1, 4):
        piece = jnp.where(lanes == m, bt[m * RG : (m + 1) * RG], piece)
    kgrad[count] = piece


def sum_kernel(
    R, T, embed_scale, weight_scale, kg, row, col, kg_out, row_out, col_out,
    kbuf, rbuf, abuf, bbuf, ksum, rcsum, kres, rcres,
    ks, kr, rs, rr, as_, ar, bs, br, k2s, k2r, r2s, r2r,
):
    N = R * T
    K, Z = kg.shape[0], row.shape[0]
    q, t = lax.axis_index("row"), lax.axis_index("diag")
    me = q * T + t

    barrier = pltpu.get_barrier_semaphore()

    def greet(p):
        @pl.when(p != me)
        def _():
            pl.semaphore_signal(barrier, inc=1, device_id={"row": p // T, "diag": p % T},
                                device_id_type=pl.DeviceIdType.MESH)
    loop(N, greet)
    pl.semaphore_wait(barrier, N - 1)

    def k1(k):
        return send(kg.at[k], kbuf.at[me], ks.at[k], kr.at[me], k // T, k % T)

    def r1(z):
        return send(row.at[z], rbuf.at[t], rs.at[z], rr.at[t], q, z)

    def a1(z):
        return send(col.at[0, z], abuf.at[q], as_.at[z], ar.at[q], q + t, z)

    def b1(z):
        return send(col.at[1, z], bbuf.at[q], bs.at[z], br.at[q], q + t + 1, z)

    def first(act):
        for k in range(K):
            @pl.when(me != k)
            def _():
                act(k1(k))
        for z in range(Z):
            @pl.when(t != z)
            def _():
                act(r1(z))

            @pl.when((q + t < R) & ((t != 0) | (z != 0)))
            def _():
                act(a1(z))

            @pl.when(q + t + 1 < R)
            def _():
                act(b1(z))

    first(lambda c: c.start())

    def got(buf, sem):
        send(buf, buf, sem, sem, q, t).wait_recv()

    def k2(p):
        return send(ksum, kres.at[me], k2s.at[p], k2r.at[me], p // T, p % T)

    def r2(p):
        return send(rcsum, rcres.at[t], r2s.at[p], r2r.at[t], q, p)

    def second(act):
        @pl.when(me < K)
        def _():
            def one(p):
                @pl.when(p != me)
                def _():
                    act(k2(p))
            loop(N, one)

        @pl.when(t < Z)
        def _():
            def one(p):
                @pl.when(p != t)
                def _():
                    act(r2(p))
            loop(T, one)

    @pl.when(me < K)
    def _():
        ksum[...] = kg[me]

        def take(p):
            @pl.when(p != me)
            def _():
                got(kbuf.at[p], kr.at[p])
                ksum[...] += kbuf[p]
        loop(N, take)
        ksum[...] = ksum[...] * weight_scale
        kres[me] = ksum[...]

    @pl.when(t < Z)
    def _():
        rcsum[0] = row[t]
        rcsum[1] = jnp.zeros_like(rcsum[1])

        def take(p):
            @pl.when(p != t)
            def _():
                got(rbuf.at[p], rr.at[p])
                rcsum[0] += rbuf[p]
        loop(T, take)

        @pl.when(t == 0)
        def _():
            rcsum[1] = col[0, 0]

        def take_col(p):
            @pl.when((p <= q) & (q - p < T) & ((p != q) | (t != 0)))
            def _():
                got(abuf.at[p], ar.at[p])
                rcsum[1] += abuf[p]

            @pl.when((p <= q - 1) & (q - 1 - p < T))
            def _():
                got(bbuf.at[p], br.at[p])
                rcsum[1] += bbuf[p]
        loop(R, take_col)
        rcsum[...] = rcsum[...] * embed_scale
        rcres[t] = rcsum[...]

    second(lambda c: c.start())
    for k in range(K):
        @pl.when(me != k)
        def _():
            got(kres.at[k], k2r.at[k])
    for z in range(Z):
        @pl.when(t != z)
        def _():
            got(rcres.at[z], r2r.at[z])
    kg_out[...] = kres[...]
    for z in range(Z):
        row_out[z * RG : (z + 1) * RG, :] = rcres[z, 0]
        col_out[z * RG : (z + 1) * RG, :] = rcres[z, 1]
    first(lambda c: c.wait_send())
    second(lambda c: c.wait_send())


def local(emb_rows, emb_cols, kernel, bias, cotangent, valid, dilation, band):
    ch, n = emb_rows.shape
    R, T = lax.axis_size("row"), lax.axis_size("diag")
    wide, ext, m = 2 * n, n + 2 * MAXDIL, MAXDIL
    bf, f32 = jnp.bfloat16, jnp.float32

    pack = jnp.concatenate(
        [emb_cols, emb_rows, jnp.broadcast_to(valid.astype(bf)[None], (16, n))], axis=0)
    cot = jnp.transpose(cotangent, (1, 0, 2))
    vmem = pl.BlockSpec(memory_space=pltpu.VMEM)
    smem = pl.BlockSpec(memory_space=pltpu.SMEM)
    dma = pltpu.SemaphoreType.DMA
    tiles = 2 * m
    edges = lambda k: pltpu.VMEM((k, ch, n), bf)
    cols, vcol, near, cot, halo = pl.pallas_call(
        functools.partial(gather_kernel, R, T),
        out_shape=(
            jax.ShapeDtypeStruct((2, ch, wide), f32),
            jax.ShapeDtypeStruct((2, RG, wide), f32),
            jax.ShapeDtypeStruct((2, ch + RG, n), f32),
            jax.ShapeDtypeStruct((ext, ch, n), bf),
            jax.ShapeDtypeStruct((ext, ch, n), bf),
        ),
        in_specs=[vmem] * 2,
        out_specs=(vmem,) * 5,
        scratch_shapes=[
            pltpu.VMEM((R + T + 3,) + pack.shape, bf),
            edges(tiles), edges(tiles), edges(tiles + 2), edges(tiles + 2), edges(m), edges(m),
            dma((R,)), dma((R,)), dma((8,)), dma((8,)),
        ],
        compiler_params=pltpu.CompilerParams(collective_id=1, has_side_effects=True),
        name="gather_kernel",
    )(pack, cot)

    blk = RG * ch
    kf = kernel.reshape(9, ch, ch)
    bias2 = bias[:, None]
    nk = (9 * ch * ch) // (RG * 128) + 1
    Z = ch // RG
    out, rsum, csum, kg = pl.pallas_call(
        pair_kernel,
        out_shape=(
            jax.ShapeDtypeStruct((n, ch, n), bf),
            jax.ShapeDtypeStruct((Z, RG, n), f32),
            jax.ShapeDtypeStruct((2, Z, RG, n), f32),
            jax.ShapeDtypeStruct((nk, RG, 128), f32),
        ),
        in_specs=[smem, smem] + [vmem] * 7,
        out_specs=(vmem,) * 4,
        scratch_shapes=[
            pltpu.VMEM((3, ext * ch, wide), bf),
            pltpu.VMEM((3, ext * ch, wide), bf),
            pltpu.VMEM((ext * ch, wide), bf),
            pltpu.VMEM((ext * ch, wide), f32),
            pltpu.VMEM((ext * ch, wide), f32),
            pltpu.VMEM((3, blk, 2 * blk), bf),
            pltpu.VMEM((3, blk, 2 * blk), bf),
            pltpu.VMEM((3, blk, 2 * blk), f32),
            pltpu.VMEM((ch, wide), f32),
            pltpu.VMEM((ch, n), f32),
            pltpu.VMEM((ch, wide), f32),
            pltpu.VMEM((ext, RG, wide), f32),
        ],
        compiler_params=pltpu.CompilerParams(vmem_limit_bytes=56 * 2**20),
        name="pair_kernel",
    )(dilation, band, near, cols, vcol, cot, halo, kf, bias2)

    tile = lambda *lead: pltpu.VMEM(lead + (RG, n), f32)
    embed_scale = float(T * n) ** -0.5
    weight_scale = float(R * n * T * n) ** -0.5
    kg, row_grad, col_grad = pl.pallas_call(
        functools.partial(sum_kernel, R, T, embed_scale, weight_scale),
        out_shape=(
            jax.ShapeDtypeStruct((nk, RG, 128), f32),
            jax.ShapeDtypeStruct((ch, n), f32),
            jax.ShapeDtypeStruct((ch, n), f32),
        ),
        in_specs=[vmem] * 3,
        out_specs=(vmem,) * 3,
        scratch_shapes=[
            tile(R * T), tile(T), tile(R), tile(R), tile(), tile(2), tile(nk), tile(Z, 2),
            dma((nk,)), dma((R * T,)), dma((Z,)), dma((T,)), dma((Z,)), dma((R,)), dma((Z,)), dma((R,)),
            dma((R * T,)), dma((nk,)), dma((T,)), dma((Z,)),
        ],
        compiler_params=pltpu.CompilerParams(collective_id=0, has_side_effects=True),
        name="sum_kernel",
    )(kg, rsum, csum)

    kgt = kg[:-1].reshape(-1, 4, ch).transpose(1, 0, 2).reshape(3, 3, ch, ch)
    bgt = kg[-1].reshape(RG, 4, ch)[:, :, 0].T.reshape(ch)
    return (
        jnp.transpose(out, (1, 0, 2)),
        row_grad,
        col_grad,
        kgt,
        bgt,
    )


def solution(mesh):
    in_specs = (
        P(None, ("grp", "row")),
        P(None, ("grp", "row")),
        P(),
        P(),
        P(None, ("grp", "row"), "diag"),
        P(("grp", "row")),
        P("grp"),
        P("grp"),
    )
    out_specs = (
        P(None, ("grp", "row"), "diag"),
        P(None, ("grp", "row")),
        P(None, ("grp", "row")),
        P("grp", None, None, None),
        P("grp"),
    )
    return jax.shard_map(local, mesh=mesh, in_specs=in_specs, out_specs=out_specs, check_vma=False)
```
